128 devices in a mesh: freq: 4 (over x), tile: 32 (over z, y, core).
Axes of the slice: x: 4, y: 4, z: 4, core: 2. Of those that a mesh axis runs over, the one named last changes fastest.
Arguments:
- u_data: bfloat16 [8, 16384, 128], P('freq', 'tile'), may hold values from -6 to 6
- u_basis: bfloat16 [8, 64, 64, 2, 48, 256], P('freq', 'tile'), may hold values from -0.25 to 0.25
- v_basis: bfloat16 [8, 64, 64, 2, 48, 256], P('freq', None, 'tile'), may hold values from -0.109375 to 0.109375
- ranks: int32 [8, 64, 64], P('freq'), may hold values from 8 to 48, as said below
- time_mask: int32 [64, 64], replicated, may hold values 0 or 1
Outputs:
- result: bfloat16 [8, 16384, 128], P('freq', 'tile')
The draws below stay inside these ranges and needn't reach their ends.
Inputs may be any that keep to these rules, and one draw needn't show every extreme that they name: For every tile and every m, ranks[2 m + 1, i, j] = 56 - ranks[2 m, i, j].
All inputs are finite; a program needn't handle non-finite values.
Results may differ from the reference program's by a relative error of at most 0.006.
Values may be sent and summed in bfloat16 or wider, within the bound.
A program may use at most 128 MiB of HBM per device.

```python
import math
import jax
import jax.numpy as jnp
from jax import lax

TILE = 256
RANK = 48
SOURCES = 64
TIMES = 64
FREQ = 8
MT = 64
NT = 64
M = 16384


def draw_ranks(key, part):
    lowest = RANK // 6
    even_ranks = jax.random.randint(jax.random.fold_in(key, 17), (FREQ // 2, MT, NT), lowest, RANK + 1, dtype=jnp.int32)
    even_ranks = even_ranks.at[0, 0, 0].set(lowest)
    odd_ranks = lowest + RANK - even_ranks
    return jnp.stack([even_ranks, odd_ranks], axis=1).reshape(FREQ, MT, NT)


def plant(values, own_key, low, largest):
    index_at = [jax.random.randint(jax.random.fold_in(own_key, axis), (), 0, length) for axis, length in enumerate(values.shape)]
    widest = values.shape.index(max(values.shape))
    next_to = index_at[:widest] + [(index_at[widest] + 1) % values.shape[widest]] + index_at[widest + 1:]
    return values.at[tuple(index_at)].set(low).at[tuple(next_to)].set(largest)


def levels(own_key, extent, split, low, top_value):
    def one(dim, shards_of):
        draws = jax.random.uniform(jax.random.fold_in(jax.random.fold_in(own_key, 6), dim), (shards_of,), jnp.float32, low / len(split), top_value / len(split))
        return jnp.repeat(jnp.exp(draws), extent[dim] // shards_of).reshape((-1,) + (1,) * (len(extent) - dim - 1))

    gain = one(*split[0])
    for cut in split[1:]:
        gain = gain * one(*cut)
    return gain


def gaussian(stream_key, extent, width, limit, split=(), held_as=jnp.bfloat16):
    values = width * jax.random.normal(stream_key, extent, jnp.float32)
    if split:
        values = values * levels(stream_key, extent, split, -0.22, 0.18)
    return jnp.clip(values, -limit, limit).astype(held_as)


def setup_inputs(seed: int = 0) -> dict:
    splits = jax.random.split(jax.random.key(seed), 6)
    return {
        "u_data": gaussian(splits[0], (FREQ, M, 2 * SOURCES), 1.0, 6.0, ((0, 4), (1, 32))),
        "u_basis": gaussian(splits[1], (FREQ, MT, NT, 2, RANK, TILE), (2 * TILE) ** -0.5, 0.25, ((0, 4), (1, 32))),
        "v_basis": gaussian(splits[2], (FREQ, MT, NT, 2, RANK, TILE), (RANK * MT) ** -0.5, 0.109375, ((0, 4), (2, 32))),
        "ranks": draw_ranks(jax.random.fold_in(splits[5], 71), 0),
        "time_mask": plant((jax.random.randint(splits[4], (TIMES, SOURCES), 0, 2) < 1).astype(jnp.int32), jax.random.fold_in(splits[4], 1), 0, 1),
    }


first_bin = 3
highest = lax.Precision.HIGHEST

def rotate(values):
    half_width = values.shape[-1] // 2
    return jnp.concatenate([-values[..., half_width:], values[..., :half_width]], axis=-1)

def conj_apply(leading, trailing):
    half_width = leading.shape[-1] // 2
    real_part = leading[..., :half_width] + trailing[..., half_width:]
    imag_part = leading[..., half_width:] - trailing[..., :half_width]
    return jnp.concatenate([real_part, imag_part], axis=-1)

def plain_apply(leading, trailing):
    half_width = leading.shape[-1] // 2
    real_part = leading[..., :half_width] - trailing[..., half_width:]
    imag_part = leading[..., half_width:] + trailing[..., :half_width]
    return jnp.concatenate([real_part, imag_part], axis=-1)

def rank_weights(tile_ranks, slot_count):
    slots = jnp.arange(slot_count, dtype=jnp.int32)
    return (slots < tile_ranks[..., None]).astype(jnp.float32)[..., None]

def dft_tables(freq_count, time_count):
    sample_ids = jnp.arange(time_count, dtype=jnp.int32)
    bin_ids = jnp.arange(freq_count, dtype=jnp.int32) + first_bin
    phase = sample_ids[:, None] * bin_ids[None, :] % time_count
    angle = 2.0 * math.pi / time_count * phase.astype(jnp.float32)
    factor = 1.0 / math.sqrt(time_count)
    return (jnp.cos(angle) * factor, jnp.sin(angle) * factor)

def adjoint_one(inputs):
    u_slab, u_tiles, v_tiles, tile_ranks = inputs
    local_rows = u_slab.reshape(MT, TILE, 2 * SOURCES).astype(jnp.float32)
    product = jnp.einsum('ijckp,ipq->ijckq', u_tiles.astype(jnp.float32), local_rows)
    coeffs = conj_apply(product[:, :, 0], product[:, :, 1]) * rank_weights(tile_ranks, RANK)
    coeffs = lax.optimization_barrier(coeffs.astype(jnp.bfloat16)).astype(jnp.float32)
    image = jnp.einsum('ijckp,ijkq->jcpq', v_tiles.astype(jnp.float32), coeffs)
    columns = plain_apply(image[:, 0], image[:, 1])
    return columns.reshape(NT * TILE, 2 * SOURCES).astype(jnp.bfloat16)

def forward_one(inputs):
    w_slab, u_tiles, v_tiles, tile_ranks = inputs
    local_cols = w_slab.reshape(NT, TILE, 2 * SOURCES).astype(jnp.float32)
    product = jnp.einsum('ijckp,jpq->ijckq', v_tiles.astype(jnp.float32), local_cols)
    coeffs = conj_apply(product[:, :, 0], product[:, :, 1])
    coeffs = lax.optimization_barrier(coeffs.astype(jnp.bfloat16)).astype(jnp.float32)
    coeffs = coeffs * rank_weights(tile_ranks, RANK)
    output = jnp.einsum('ijckp,ijkq->icpq', u_tiles.astype(jnp.float32), coeffs)
    rows_out = plain_apply(output[:, 0], output[:, 1])
    return rows_out.reshape(MT * TILE, 2 * SOURCES).astype(jnp.bfloat16)

def reference(u_data, u_basis, v_basis, ranks, time_mask):
    adjoint = lax.map(adjoint_one, (u_data, u_basis, v_basis, ranks))
    cos_table, sin_table = dft_tables(FREQ, TIMES)
    kept = time_mask.astype(jnp.float32)
    kept = jnp.concatenate([kept, kept], axis=-1)

    def mix_block(block):
        values = block.astype(jnp.float32)
        signal = jnp.einsum('tf,fnq->tnq', cos_table, values, precision=highest)
        signal = signal + jnp.einsum('tf,fnq->tnq', sin_table, rotate(values), precision=highest)
        signal = signal * kept[:, None, :]
        result = jnp.einsum('tf,tnq->fnq', cos_table, signal, precision=highest)
        result = result - jnp.einsum('tf,tnq->fnq', sin_table, rotate(signal), precision=highest)
        return result.astype(jnp.bfloat16)
    blocks = adjoint.reshape(FREQ, NT, TILE, 2 * SOURCES).transpose(1, 0, 2, 3)
    mixed = lax.map(mix_block, blocks).transpose(1, 0, 2, 3).reshape(FREQ, NT * TILE, 2 * SOURCES)
    return lax.map(forward_one, (mixed, u_basis, v_basis, ranks))
```

```python
import math

import jax
import jax.numpy as jnp
import numpy as np
from jax import lax
from jax.experimental import pallas as pl
from jax.experimental.pallas import tpu as pltpu
from jax.sharding import PartitionSpec as P

MESH = pl.DeviceIdType.MESH
PEERS = 32
GROUP = 4
GROUPS = PEERS // GROUP
SLOTS = 48
PAIR = 56
WIDTH = 128
TILE = 256
LAGS = 15


def lag_table(times):
    table = np.zeros((times, 128), np.float32)
    t = np.arange(times)
    for lag in range(-7, 8):
        angle = 2.0 * math.pi * ((lag * t) % times) / times
        table[:, 2 * (lag + 7)] = np.cos(angle) / times
        table[:, 2 * (lag + 7) + 1] = np.sin(angle) / times
    return table


def place(slot, sign):
    me = lax.axis_index("tile")
    offset = (13 * slot) % PEERS
    z = (me // 8 + sign * (offset // 8) + 4) % 4
    y = ((me // 2) % 4 + sign * ((offset // 2) % 4) + 4) % 4
    c = (me % 2 + offset % 2) % 2
    return z * 8 + y * 2 + c


def flip8(x):
    rows = lax.broadcasted_iota(jnp.int32, (8, WIDTH), 0)
    return jnp.take_along_axis(x, 7 - rows, axis=0)


def pack(first, second, rank):
    rows = lax.broadcasted_iota(jnp.int32, (8, WIDTH), 0)
    parts = [first[0:8]]
    for v in range(1, 6):
        other = flip8(second[8 * (6 - v) : 8 * (6 - v) + 8])
        parts.append(jnp.where(rows + 8 * v < rank, first[8 * v : 8 * v + 8], other))
    parts.append(flip8(second[0:8]))
    return parts


def unpack(packed, rank):
    rows = lax.broadcasted_iota(jnp.int32, (8, WIDTH), 0)
    first, second = [], []
    for v in range(6):
        first.append(jnp.where(rows + 8 * v < rank, packed[v], 0.0))
        second.append(jnp.where(rows + 8 * v < PAIR - rank, flip8(packed[6 - v]), 0.0))
    return jnp.concatenate(first, axis=0), jnp.concatenate(second, axis=0)


def turned(x):
    lanes = lax.broadcasted_iota(jnp.int32, x.shape, 1)
    rolled = pltpu.roll(x, WIDTH // 2, 1)
    return jnp.where(lanes < WIDTH // 2, -rolled, rolled)


def kernel(
    u_hbm, ub_hbm, vb_hbm, ranks_hbm, mask_hbm, table_hbm, out_ref,
    u_buf, ub, vb, ranks, mask, table, weights, lags,
    send, recv, z_send, z_recv, z_acc, r_acc,
    in_sem, u_sem, v_sem, send_sem, recv_sem, zs_sem, zr_sem,
):
    me = lax.axis_index("tile")
    fx = lax.axis_index("freq")
    barrier = pltpu.get_barrier_semaphore()

    def greet(slot, carry):
        pl.semaphore_signal(barrier, inc=1, device_id={"tile": place(slot, 1)}, device_id_type=MESH)
        return carry

    lax.fori_loop(1, PEERS, greet, 0)
    for dx in (1, 2, 3):
        pl.semaphore_signal(barrier, inc=1, device_id={"freq": (fx + dx) % 4}, device_id_type=MESH)

    copies = [
        pltpu.make_async_copy(u_hbm, u_buf, in_sem.at[0]),
        pltpu.make_async_copy(ranks_hbm, ranks, in_sem.at[1]),
        pltpu.make_async_copy(mask_hbm, mask, in_sem.at[2]),
        pltpu.make_async_copy(table_hbm, table, in_sem.at[3]),
    ]
    for copy in copies:
        copy.start()

    def u_copy(jj, slot):
        j = 2 * place(slot, 1) + jj
        return pltpu.make_async_copy(ub_hbm.at[:, :, j], ub.at[:, :, j], u_sem.at[jj, slot])

    def v_copy(jj, slot):
        i = 2 * place(slot, -1)
        return pltpu.make_async_copy(
            vb_hbm.at[:, pl.ds(i, 2), jj], vb.at[:, pl.ds(i, 2), jj], v_sem.at[jj, slot]
        )

    for jj in range(2):
        def fetch_u(slot, carry):
            u_copy(jj, slot).start()
            return carry
        lax.fori_loop(0, PEERS, fetch_u, 0)
    for jj in range(2):
        def fetch_v(slot, carry):
            v_copy(jj, slot).start()
            return carry
        lax.fori_loop(0, PEERS, fetch_v, 0)

    def remote(stage, jj, slot):
        return pltpu.make_async_remote_copy(
            src_ref=send.at[stage, jj, slot],
            dst_ref=recv.at[stage, jj, slot],
            send_sem=send_sem.at[stage, jj, slot],
            recv_sem=recv_sem.at[stage, jj, slot],
            device_id={"tile": place(slot, 1)},
            device_id_type=MESH,
        )

    def stay(stage, jj):
        return pltpu.make_async_copy(
            send.at[stage, jj, 0], recv.at[stage, jj, 0], recv_sem.at[stage, jj, 0]
        )

    def dispatch(stage, jj, group):
        @pl.when(group == 0)
        def _():
            stay(stage, jj).start()

        @pl.when(group > 0)
        def _():
            remote(stage, jj, GROUP * group).start()

        for k in range(1, GROUP):
            remote(stage, jj, GROUP * group + k).start()

    def arrive(stage, jj, group):
        @pl.when(group == 0)
        def _():
            stay(stage, jj).wait()

        @pl.when(group > 0)
        def _():
            remote(stage, jj, GROUP * group).wait_recv()

        for k in range(1, GROUP):
            remote(stage, jj, GROUP * group + k).wait_recv()

    copies[0].wait()
    for f in range(2):
        for i in range(2):
            x = u_buf[f, 256 * i : 256 * i + 256, :].astype(jnp.float32)
            weights[f, i, 0:256, :] = x.astype(jnp.bfloat16)
            weights[f, i, 256:512, :] = (-turned(x)).astype(jnp.bfloat16)
    copies[1].wait()

    def product(tiles, f, i):
        real = jnp.concatenate([t[0] for t in tiles], axis=0)
        imag = jnp.concatenate([t[1] for t in tiles], axis=0)
        lhs = jnp.concatenate([real, imag], axis=1)
        return jnp.dot(lhs, weights[f, i], preferred_element_type=jnp.float32)

    def emit(stage, jj, group, parts):
        for k in range(GROUP):
            block = jnp.concatenate(parts[0][k] + parts[1][k], axis=0)
            send[stage, jj, GROUP * group + k] = block.astype(jnp.bfloat16)

    def adjoint(jj, group, carry):
        where = [place(GROUP * group + k, 1) for k in range(GROUP)]
        for k in range(GROUP):
            u_copy(jj, GROUP * group + k).wait()
        parts = []
        for i in range(2):
            both = [product([ub[f, i, 2 * d + jj] for d in where], f, i) for f in range(2)]
            parts.append([
                pack(both[0][48 * k : 48 * k + 48], both[1][48 * k : 48 * k + 48],
                     ranks[0, 2 * me + i, 2 * where[k] + jj])
                for k in range(GROUP)
            ])

        @pl.when(group > 0)
        def _():
            dispatch(0, jj, group - 1)

        emit(0, jj, group, parts)
        return carry

    adjoint(0, 0, 0)
    pl.semaphore_wait(barrier, PEERS - 1 + 3)
    lax.fori_loop(1, GROUPS, lambda g, c: adjoint(0, g, c), 0)
    dispatch(0, 0, GROUPS - 1)
    lax.fori_loop(0, GROUPS, lambda g, c: adjoint(1, g, c), 0)
    dispatch(0, 1, GROUPS - 1)

    copies[2].wait()
    copies[3].wait()
    kept = mask[...].astype(jnp.float32)
    mixing = lax.dot_general(
        kept, table[...], (((0,), (0,)), ((), ())),
        precision=lax.Precision.HIGHEST, preferred_element_type=jnp.float32,
    )
    for lag in range(LAGS):
        for part in range(2):
            column = mixing[:, 2 * lag + part : 2 * lag + part + 1]
            lags[lag, part] = jnp.broadcast_to(column, (64, 128))

    def gather(jj, group, carry):
        whence = [place(GROUP * group + k, -1) for k in range(GROUP)]
        arrive(0, jj, group)
        stacks = [[], []]
        for k in range(GROUP):
            v_copy(jj, GROUP * group + k).wait()
            block = recv[0, jj, GROUP * group + k].astype(jnp.float32)
            for i in range(2):
                pieces = [block[56 * i + 8 * v : 56 * i + 8 * v + 8] for v in range(7)]
                pair = unpack(pieces, ranks[0, 2 * whence[k] + i, 2 * me + jj])
                for f in range(2):
                    stacks[f] += [pair[f], turned(pair[f])]
        for f in range(2):
            lhs = jnp.concatenate([s.astype(jnp.bfloat16) for s in stacks[f]], axis=0)
            rhs = jnp.concatenate(
                [vb[f, 2 * d + i, jj, c] for d in whence for i in range(2) for c in range(2)], axis=0
            )
            z_acc[f] += lax.dot_general(
                lhs, rhs, (((0,), (0,)), ((), ())), preferred_element_type=jnp.float32
            )
        return carry

    def clear():
        z_acc[...] = jnp.zeros_like(z_acc)

    def z_copy(jj, dx):
        return pltpu.make_async_remote_copy(
            src_ref=z_send.at[jj],
            dst_ref=z_recv.at[jj, dx - 1],
            send_sem=zs_sem.at[jj, dx - 1],
            recv_sem=zr_sem.at[jj, dx - 1],
            device_id={"freq": (fx + dx) % 4},
            device_id_type=MESH,
        )

    def share(jj):
        z_send[jj] = z_acc[...].astype(jnp.bfloat16)
        for dx in (2, 1, 3):
            z_copy(jj, dx).start()

    def mix(jj):
        for dx in (1, 3, 2):
            z_copy(jj, dx).wait_recv()
        for f in range(2):
            halves = []
            for h in range(2):
                cut = slice(128 * h, 128 * h + 128)
                real = jnp.zeros((64, 128), jnp.float32)
                imag = jnp.zeros((64, 128), jnp.float32)
                for dx in range(4):
                    for g in range(2):
                        held = z_send.at[jj] if dx == 0 else z_recv.at[jj, dx - 1]
                        zr = held[g, 0:64, cut].astype(jnp.float32)
                        zi = held[g, 64:128, cut].astype(jnp.float32)
                        lag = 2 * ((fx - dx + 4) % 4 - fx) + g - f + 7
                        cr = lags[lag, 0]
                        ci = lags[lag, 1]
                        real += cr * zr - ci * zi
                        imag += cr * zi + ci * zr
                halves.append((real, imag))
            for h in range(2):
                real, imag = halves[h]
                straight = jnp.concatenate([real, imag], axis=0)
                crossed = jnp.concatenate([imag, -real], axis=0)
                weights[f, 0, 128 * h : 128 * h + 128, :] = straight.T.astype(jnp.bfloat16)
                weights[f, 0, 256 + 128 * h : 384 + 128 * h, :] = crossed.T.astype(jnp.bfloat16)

    def forward(jj, group, carry):
        where = [place(GROUP * group + k, 1) for k in range(GROUP)]
        parts = []
        for i in range(2):
            both = [product([vb[f, 2 * d + i, jj] for d in where], f, 0) for f in range(2)]
            parts.append([
                pack(both[0][48 * k : 48 * k + 48], both[1][48 * k : 48 * k + 48],
                     ranks[0, 2 * where[k] + i, 2 * me + jj])
                for k in range(GROUP)
            ])

        @pl.when(group > 0)
        def _():
            dispatch(1, jj, group - 1)

        emit(1, jj, group, parts)
        return carry

    def finish(jj, group, carry):
        whence = [place(GROUP * group + k, -1) for k in range(GROUP)]
        arrive(1, jj, group)
        stacks = [[[], []], [[], []]]
        for k in range(GROUP):
            block = recv[1, jj, GROUP * group + k].astype(jnp.float32)
            for i in range(2):
                pieces = [block[56 * i + 8 * v : 56 * i + 8 * v + 8] for v in range(7)]
                pair = unpack(pieces, ranks[0, 2 * me + i, 2 * whence[k] + jj])
                for f in range(2):
                    stacks[f][i] += [pair[f], turned(pair[f])]
        for f in range(2):
            for i in range(2):
                lhs = jnp.concatenate([s.astype(jnp.bfloat16) for s in stacks[f][i]], axis=0)
                rhs = jnp.concatenate(
                    [ub[f, i, 2 * d + jj, c] for d in whence for c in range(2)], axis=0
                )
                r_acc[f, i] += lax.dot_general(
                    lhs, rhs, (((0,), (0,)), ((), ())), preferred_element_type=jnp.float32
                )
        return carry

    clear()
    r_acc[...] = jnp.zeros_like(r_acc)
    lax.fori_loop(0, GROUPS, lambda g, c: gather(0, g, c), 0)
    share(0)
    clear()
    ahead = 5
    lax.fori_loop(0, ahead, lambda g, c: gather(1, g, c), 0)
    mix(0)
    lax.fori_loop(0, GROUPS, lambda g, c: forward(0, g, c), 0)
    dispatch(1, 0, GROUPS - 1)
    lax.fori_loop(ahead, GROUPS, lambda g, c: gather(1, g, c), 0)
    share(1)
    lax.fori_loop(0, ahead, lambda g, c: finish(0, g, c), 0)
    mix(1)
    lax.fori_loop(0, GROUPS, lambda g, c: forward(1, g, c), 0)
    dispatch(1, 1, GROUPS - 1)
    lax.fori_loop(ahead, GROUPS, lambda g, c: finish(0, g, c), 0)
    lax.fori_loop(0, GROUPS, lambda g, c: finish(1, g, c), 0)
    for f in range(2):
        for i in range(2):
            out_ref[f, 256 * i : 256 * i + 256, :] = r_acc[f, i].T.astype(jnp.bfloat16)

    for stage in range(2):
        for jj in range(2):
            def drain(slot, carry):
                remote(stage, jj, slot).wait_send()
                return carry
            lax.fori_loop(1, PEERS, drain, 0)
    for jj in range(2):
        for dx in (1, 2, 3):
            z_copy(jj, dx).wait_send()


def local(u_data, u_basis, v_basis, ranks, time_mask):
    times = time_mask.shape[0]
    table = jnp.asarray(lag_table(times))
    anywhere = pl.BlockSpec(memory_space=pl.ANY)
    bf16, f32 = jnp.bfloat16, jnp.float32
    return pl.pallas_call(
        kernel,
        out_shape=jax.ShapeDtypeStruct(u_data.shape, bf16),
        in_specs=[anywhere] * 6,
        out_specs=pl.BlockSpec(memory_space=pltpu.VMEM),
        scratch_shapes=[
            pltpu.VMEM(u_data.shape, bf16),
            pltpu.VMEM(u_basis.shape, bf16),
            pltpu.VMEM(v_basis.shape, bf16),
            pltpu.SMEM(ranks.shape, jnp.int32),
            pltpu.VMEM(time_mask.shape, jnp.int32),
            pltpu.VMEM(table.shape, f32),
            pltpu.VMEM((2, 2, 2 * TILE, WIDTH), bf16),
            pltpu.VMEM((LAGS, 2, 64, 128), f32),
            pltpu.VMEM((2, 2, PEERS, 2 * PAIR, WIDTH), bf16),
            pltpu.VMEM((2, 2, PEERS, 2 * PAIR, WIDTH), bf16),
            pltpu.VMEM((2, 2, WIDTH, TILE), bf16),
            pltpu.VMEM((2, 3, 2, WIDTH, TILE), bf16),
            pltpu.VMEM((2, WIDTH, TILE), f32),
            pltpu.VMEM((2, 2, WIDTH, TILE), f32),
            pltpu.SemaphoreType.DMA((4,)),
            pltpu.SemaphoreType.DMA((2, PEERS)),
            pltpu.SemaphoreType.DMA((2, PEERS)),
            pltpu.SemaphoreType.DMA((2, 2, PEERS)),
            pltpu.SemaphoreType.DMA((2, 2, PEERS)),
            pltpu.SemaphoreType.DMA((2, 3)),
            pltpu.SemaphoreType.DMA((2, 3)),
        ],
        compiler_params=pltpu.CompilerParams(
            collective_id=0, has_side_effects=True, vmem_limit_bytes=63 * 1024 * 1024
        ),
        name="fused",
    )(u_data, u_basis, v_basis, ranks, time_mask, table)


def solution(mesh):
    placed = (
        P("freq", "tile", None),
        P("freq", "tile", None, None, None, None),
        P("freq", None, "tile", None, None, None),
        P("freq", None, None),
        P(),
    )
    return jax.shard_map(
        local, mesh=mesh, in_specs=placed, out_specs=P("freq", "tile", None), check_vma=False
    )
```

```python
import math

import jax
import jax.numpy as jnp
import numpy as np
from jax import lax
from jax.experimental import pallas as pl
from jax.experimental.pallas import tpu as pltpu
from jax.sharding import PartitionSpec as P

MESH = pl.DeviceIdType.MESH
PEERS = 32
GROUP = 4
GROUPS = PEERS // GROUP
SLOTS = 48
PAIR = 56
WIDTH = 128
TILE = 256
LAGS = 15


def lag_table(times):
    table = np.zeros((times, 128), np.float32)
    t = np.arange(times)
    for lag in range(-7, 8):
        angle = 2.0 * math.pi * ((lag * t) % times) / times
        table[:, 2 * (lag + 7)] = np.cos(angle) / times
        table[:, 2 * (lag + 7) + 1] = np.sin(angle) / times
    return table


SELF = PEERS - 1


def quot(a, b):
    return a // b if isinstance(a, int) else lax.div(a, b)


def mod(a, b):
    return a % b if isinstance(a, int) else lax.rem(a, b)


def offset(group, k):
    half = quot(group, 4)
    return mod(1 + group, 4), 2 + half if k < 2 else 1 - half, 1 - k % 2


def flip8(x):
    rows = lax.broadcasted_iota(jnp.int32, (8, WIDTH), 0)
    return jnp.take_along_axis(x, 7 - rows, axis=0)


def pack(first, second, rank):
    rows = lax.broadcasted_iota(jnp.int32, (8, WIDTH), 0)
    parts = [first[0:8]]
    for v in range(1, 6):
        other = flip8(second[8 * (6 - v) : 8 * (6 - v) + 8])
        parts.append(jnp.where(rows + 8 * v < rank, first[8 * v : 8 * v + 8], other))
    parts.append(flip8(second[0:8]))
    return parts


def unpack(packed, rank):
    rows = lax.broadcasted_iota(jnp.int32, (8, WIDTH), 0)
    first, second = [], []
    for v in range(6):
        first.append(jnp.where(rows + 8 * v < rank, packed[v], 0.0))
        second.append(jnp.where(rows + 8 * v < PAIR - rank, flip8(packed[6 - v]), 0.0))
    return jnp.concatenate(first, axis=0), jnp.concatenate(second, axis=0)


def turned(x):
    lanes = lax.broadcasted_iota(jnp.int32, x.shape, 1)
    rolled = pltpu.roll(x, WIDTH // 2, 1)
    return jnp.where(lanes < WIDTH // 2, -rolled, rolled)


def kernel(
    u_hbm, ub_hbm, vb_hbm, ranks_hbm, mask_hbm, table_hbm, out_ref,
    u_buf, ub, vb, ranks, mask, table, weights, lags, prod, side, turns,
    send, recv, z_send, z_recv, z_acc, r_acc,
    in_sem, u_sem, v_sem, send_sem, recv_sem, zs_sem, zr_sem,
):
    me = lax.axis_index("tile")
    fx = lax.axis_index("freq")
    z, y, c = quot(me, 8), mod(quot(me, 2), 4), mod(me, 2)
    zs = [mod(z + d, 4) * 8 for d in range(4)]
    ys = [mod(y + d, 4) * 2 for d in range(4)]
    cs = [c, 1 - c]
    xs = [mod(fx + d, 4) for d in range(4)]
    scope = jax.named_scope

    barrier = pltpu.get_barrier_semaphore()
    for slot in range(SELF):
        dz, dy, dc = offset(slot // GROUP, slot % GROUP)
        pl.semaphore_signal(
            barrier, inc=1, device_id={"tile": zs[dz] + ys[dy] + cs[dc]}, device_id_type=MESH
        )
    for dx in (1, 2, 3):
        pl.semaphore_signal(barrier, inc=1, device_id={"freq": xs[dx]}, device_id_type=MESH)

    copies = [
        pltpu.make_async_copy(u_hbm, u_buf, in_sem.at[0]),
        pltpu.make_async_copy(ranks_hbm, ranks, in_sem.at[1]),
        pltpu.make_async_copy(mask_hbm, mask, in_sem.at[2]),
        pltpu.make_async_copy(table_hbm, table, in_sem.at[3]),
    ]

    def u_copy(dz):
        cut = pl.ds(pl.multiple_of(2 * zs[dz], 16), 16)
        return pltpu.make_async_copy(ub_hbm.at[:, :, cut], ub.at[:, :, cut], u_sem.at[dz])

    def v_copy(dz):
        cut = pl.ds(pl.multiple_of(2 * zs[(4 - dz) % 4], 16), 16)
        return pltpu.make_async_copy(vb_hbm.at[:, cut], vb.at[:, cut], v_sem.at[dz])

    copies[0].start()
    copies[1].start()
    for dz in (1, 2, 3, 0):
        u_copy(dz).start()
    copies[2].start()
    copies[3].start()

    def targets(group):
        spots = []
        for k in range(GROUP):
            dz, dy, dc = offset(group, k)
            spots.append(mod(z + dz, 4) * 8 + mod(y + dy, 4) * 2 + cs[dc])
        return spots

    def sources(group):
        spots = []
        for k in range(GROUP):
            dz, dy, dc = offset(group, k)
            spots.append(mod(z + 4 - dz, 4) * 8 + mod(y + 4 - dy, 4) * 2 + cs[dc])
        return spots

    def dispatch(stage, jj, group, count=GROUP):
        where = targets(group)
        for k in range(count):
            slot = GROUP * group + k
            pltpu.make_async_remote_copy(
                src_ref=send.at[stage, jj, slot],
                dst_ref=recv.at[stage, jj, slot],
                send_sem=send_sem.at[stage, jj],
                recv_sem=recv_sem.at[stage, jj, group],
                device_id={"tile": where[k]},
                device_id_type=MESH,
            ).start()

    def bulk(stage, jj, first, count, sem):
        cut = pl.ds(first, count)
        return pltpu.make_async_copy(send.at[stage, jj, cut], recv.at[stage, jj, cut], sem)

    def arrive(stage, jj, group, count=GROUP):
        bulk(stage, jj, GROUP * group, count, recv_sem.at[stage, jj, group]).wait()

    with scope("u_wait"):
        copies[0].wait()
    for f in range(2):
        for i in range(2):
            x = u_buf[f, 256 * i : 256 * i + 256, :]
            weights[f, i, 0:256, :] = x
            weights[f, i, 256:512, :] = (-turned(x.astype(jnp.float32))).astype(jnp.bfloat16)
    copies[1].wait()

    def multiply(group, tile, weight):
        where = targets(group)
        for i in range(2):
            for f in range(2):
                tiles = [tile(f, i, d) for d in where]
                real = jnp.concatenate([t[0] for t in tiles], axis=0)
                imag = jnp.concatenate([t[1] for t in tiles], axis=0)
                lhs = jnp.concatenate([real, imag], axis=1)
                prod[i, f] = jnp.dot(lhs, weight(f, i), preferred_element_type=jnp.float32)

    def emit(stage, jj, group, rank):
        where = targets(group)
        for k in range(GROUP):
            cut = slice(48 * k, 48 * k + 48)
            parts = []
            for i in range(2):
                parts += pack(prod[i, 0, cut], prod[i, 1, cut], rank(i, where[k]))
            send[stage, jj, GROUP * group + k] = jnp.concatenate(parts, axis=0).astype(jnp.bfloat16)

    def coefficients(stage, jj, tile, weight, rank, before=None, between=None, paced=False):
        multiply(0, tile, weight)
        if before is not None:
            before(1)
        emit(stage, jj, 0, rank)
        multiply(1, tile, weight)

        def step(group, carry):
            if not paced:
                dispatch(stage, jj, group - 2)
            emit(stage, jj, group - 1, rank)
            multiply(group, tile, weight)
            return carry

        first = 2
        if before is not None:
            before(2)
            step(2, 0)
            before(3)
            first = 3
        if between is not None:
            lax.fori_loop(first, GROUPS // 2 + 1, step, 0)
            first = GROUPS // 2 + 1
            between()
        lax.fori_loop(first, GROUPS, step, 0)
        if not paced:
            dispatch(stage, jj, GROUPS - 2)
        emit(stage, jj, GROUPS - 1, rank)
        if not paced:
            dispatch(stage, jj, GROUPS - 1, GROUP - 1)

    def adjoint(jj, **marks):
        coefficients(
            0, jj,
            lambda f, i, d: ub[f, i, 2 * d + jj],
            lambda f, i: weights[f, i],
            lambda i, d: ranks[0, 2 * me + i, 2 * d + jj],
            **marks,
        )

    def forward(jj, **marks):
        coefficients(
            1, jj,
            lambda f, i, d: vb[f, 2 * d + i, jj],
            lambda f, i: weights[f, 0],
            lambda i, d: ranks[0, 2 * d + i, 2 * me + jj],
            **marks,
        )

    def loaded(group):
        if group == 1:
            u_copy(2).wait()
        elif group == 2:
            u_copy(3).wait()
            with scope("barrier"):
                pl.semaphore_wait(barrier, PEERS - 1 + 3)
        else:
            u_copy(0).wait()
            for dz in (1, 2, 3, 0):
                v_copy(dz).start()

    with scope("adj0"):
        u_copy(1).wait()
        adjoint(0, before=loaded)
    with scope("adj1"):
        adjoint(1, paced=True)

    copies[2].wait()
    copies[3].wait()
    kept = mask[...].astype(jnp.float32)
    mixing = lax.dot_general(
        kept, table[...], (((0,), (0,)), ((), ())),
        precision=lax.Precision.HIGHEST, preferred_element_type=jnp.float32,
    )
    for lag in range(LAGS):
        for part in range(2):
            column = mixing[:, 2 * lag + part : 2 * lag + part + 1]
            lags[lag, part] = jnp.broadcast_to(column, (64, 128))

    def crossed(x):
        half = WIDTH // 2
        return jnp.concatenate([-x[half:], x[:half]], axis=0)

    def opened(stage, jj, slot, rank):
        block = (send if slot is None else recv)[stage, jj, SELF if slot is None else slot]
        block = block.astype(jnp.float32)
        pairs = []
        for i in range(2):
            pieces = [block[56 * i + 8 * v : 56 * i + 8 * v + 8] for v in range(7)]
            pairs.append(unpack(pieces, rank(i)))
        return pairs

    def slot_of(group, k, last):
        return None if last and k == GROUP - 1 else GROUP * group + k

    def take(jj, group, last=False):
        whence = sources(group)
        stacks = [[], []]
        for k in range(GROUP):
            pairs = opened(
                0, jj, slot_of(group, k, last), lambda i: ranks[0, 2 * whence[k] + i, 2 * me + jj]
            )
            for i in range(2):
                for f in range(2):
                    stacks[f].append(pairs[i][f].astype(jnp.bfloat16))
        for f in range(2):
            side[f] = jnp.concatenate(stacks[f], axis=0).T

    def add(jj, group):
        whence = sources(group)
        for f in range(2):
            held = side[f]
            lhs = jnp.concatenate([held, crossed(held)], axis=1)
            rhs = jnp.concatenate(
                [vb[f, 2 * d + i, jj, c] for c in range(2) for d in whence for i in range(2)], axis=0
            )
            z_acc[f] += jnp.dot(lhs, rhs, preferred_element_type=jnp.float32)

    def take_back(jj, group, last=False):
        whence = sources(group)
        stacks = [[[], []], [[], []]]
        for k in range(GROUP):
            pairs = opened(
                1, jj, slot_of(group, k, last), lambda i: ranks[0, 2 * me + i, 2 * whence[k] + jj]
            )
            for i in range(2):
                for f in range(2):
                    stacks[f][i].append(pairs[i][f].astype(jnp.bfloat16))
        for f in range(2):
            for i in range(2):
                turns[f, i] = jnp.concatenate(stacks[f][i], axis=0).T

    def add_back(jj, group):
        whence = sources(group)
        for f in range(2):
            for i in range(2):
                held = turns[f, i]
                total = r_acc[f, i]
                for c, lhs in enumerate((held, crossed(held))):
                    rhs = jnp.concatenate([ub[f, i, 2 * d + jj, c] for d in whence], axis=0)
                    total = total + jnp.dot(lhs, rhs, preferred_element_type=jnp.float32)
                r_acc[f, i] = total

    def gather(stage, jj, first, stop, then=None):
        unpack_group, add_group = ((take, add), (take_back, add_back))[stage]
        if first == 0:
            arrive(stage, jj, 0)
            if then is not None:
                dispatch(*then, 0)
            unpack_group(jj, 0)
            first = 1

        def step(group, carry):
            arrive(stage, jj, group)
            if then is not None:
                dispatch(*then, group)
            add_group(jj, group - 1)
            unpack_group(jj, group)
            return carry

        lax.fori_loop(first, min(stop, GROUPS - 1), step, 0)
        if stop == GROUPS:
            arrive(stage, jj, GROUPS - 1, GROUP - 1)
            if then is not None:
                dispatch(*then, GROUPS - 1, GROUP - 1)
            add_group(jj, GROUPS - 2)
            unpack_group(jj, GROUPS - 1, True)
            add_group(jj, GROUPS - 1)

    def clear():
        z_acc[...] = jnp.zeros_like(z_acc)

    def z_copy(jj, dx):
        return pltpu.make_async_remote_copy(
            src_ref=z_send.at[jj],
            dst_ref=z_recv.at[jj, dx - 1],
            send_sem=zs_sem.at[jj, dx - 1],
            recv_sem=zr_sem.at[jj, dx - 1],
            device_id={"freq": xs[dx]},
            device_id_type=MESH,
        )

    def share(jj):
        z_send[jj] = z_acc[...].astype(jnp.bfloat16)
        for dx in (2, 1, 3):
            z_copy(jj, dx).start()

    def mix(jj):
        with scope(f"mixwait{jj}"):
            for dx in (1, 3, 2):
                z_copy(jj, dx).wait_recv()
        for f in range(2):
            for h in range(2):
                cut = slice(128 * h, 128 * h + 128)
                real = jnp.zeros((64, 128), jnp.float32)
                imag = jnp.zeros((64, 128), jnp.float32)
                for dx in range(4):
                    for g in range(2):
                        held = z_send.at[jj] if dx == 0 else z_recv.at[jj, dx - 1]
                        zr = held[g, 0:64, cut].astype(jnp.float32)
                        zi = held[g, 64:128, cut].astype(jnp.float32)
                        lag = 2 * (xs[(4 - dx) % 4] - fx) + g - f + 7
                        cr = lags[lag, 0]
                        ci = lags[lag, 1]
                        real += cr * zr - ci * zi
                        imag += cr * zi + ci * zr
                straight = jnp.concatenate([real, imag], axis=0)
                swapped = jnp.concatenate([imag, -real], axis=0)
                weights[f, 0, 128 * h : 128 * h + 128, :] = straight.T.astype(jnp.bfloat16)
                weights[f, 0, 256 + 128 * h : 384 + 128 * h, :] = swapped.T.astype(jnp.bfloat16)

    clear()
    r_acc[...] = jnp.zeros_like(r_acc)
    for dz in (1, 2, 3, 0):
        v_copy(dz).wait()
    with scope("gather0"):
        gather(0, 0, 0, GROUPS, then=(0, 1))
    with scope("share0"):
        share(0)
        clear()
    with scope("gather1a"):
        gather(0, 1, 0, 3)

    def rest():
        with scope("gather1b"):
            gather(0, 1, 3, GROUPS)
        with scope("share1"):
            share(1)

    with scope("mix0"):
        mix(0)
    with scope("forward0"):
        forward(0)
    rest()
    with scope("finish0a"):
        pass
    with scope("mix1"):
        mix(1)
    with scope("forward1"):
        forward(1)
    with scope("finish0b"):
        gather(1, 0, 0, GROUPS)
    with scope("finish1"):
        gather(1, 1, 0, GROUPS)
    with scope("tail"):
        for f in range(2):
            for i in range(2):
                out_ref[f, 256 * i : 256 * i + 256, :] = r_acc[f, i].T.astype(jnp.bfloat16)
        for stage in range(2):
            for jj in range(2):
                bulk(stage, jj, 0, SELF, send_sem.at[stage, jj]).wait()
        for jj in range(2):
            for dx in (1, 2, 3):
                z_copy(jj, dx).wait_send()


def local(u_data, u_basis, v_basis, ranks, time_mask):
    times = time_mask.shape[0]
    table = jnp.asarray(lag_table(times))
    anywhere = pl.BlockSpec(memory_space=pl.ANY)
    bf16, f32 = jnp.bfloat16, jnp.float32
    return pl.pallas_call(
        kernel,
        out_shape=jax.ShapeDtypeStruct(u_data.shape, bf16),
        in_specs=[anywhere] * 6,
        out_specs=pl.BlockSpec(memory_space=pltpu.VMEM),
        scratch_shapes=[
            pltpu.VMEM(u_data.shape, bf16),
            pltpu.VMEM(u_basis.shape, bf16),
            pltpu.VMEM(v_basis.shape, bf16),
            pltpu.SMEM(ranks.shape, jnp.int32),
            pltpu.VMEM(time_mask.shape, jnp.int32),
            pltpu.VMEM(table.shape, f32),
            pltpu.VMEM((2, 2, 2 * TILE, WIDTH), bf16),
            pltpu.VMEM((LAGS, 2, 64, 128), f32),
            pltpu.VMEM((2, 2, GROUP * SLOTS, WIDTH), f32),
            pltpu.VMEM((2, WIDTH, 2 * GROUP * SLOTS), bf16),
            pltpu.VMEM((2, 2, WIDTH, GROUP * SLOTS), bf16),
            pltpu.VMEM((2, 2, PEERS, 2 * PAIR, WIDTH), bf16),
            pltpu.VMEM((2, 2, PEERS, 2 * PAIR, WIDTH), bf16),
            pltpu.VMEM((2, 2, WIDTH, TILE), bf16),
            pltpu.VMEM((2, 3, 2, WIDTH, TILE), bf16),
            pltpu.VMEM((2, WIDTH, TILE), f32),
            pltpu.VMEM((2, 2, WIDTH, TILE), f32),
            pltpu.SemaphoreType.DMA((4,)),
            pltpu.SemaphoreType.DMA((4,)),
            pltpu.SemaphoreType.DMA((4,)),
            pltpu.SemaphoreType.DMA((2, 2)),
            pltpu.SemaphoreType.DMA((2, 2, GROUPS)),
            pltpu.SemaphoreType.DMA((2, 3)),
            pltpu.SemaphoreType.DMA((2, 3)),
        ],
        compiler_params=pltpu.CompilerParams(
            collective_id=0, has_side_effects=True, vmem_limit_bytes=63 * 1024 * 1024
        ),
        name="fused",
    )(u_data, u_basis, v_basis, ranks, time_mask, table)


def solution(mesh):
    placed = (
        P("freq", "tile", None),
        P("freq", "tile", None, None, None, None),
        P("freq", None, "tile", None, None, None),
        P("freq", None, None),
        P(),
    )
    return jax.shard_map(
        local, mesh=mesh, in_specs=placed, out_specs=P("freq", "tile", None), check_vma=False
    )
```

```python
import math

import jax
import jax.numpy as jnp
import numpy as np
from jax import lax
from jax.experimental import pallas as pl
from jax.experimental.pallas import tpu as pltpu
from jax.sharding import PartitionSpec as P

MESH = pl.DeviceIdType.MESH
PEERS = 32
LEAD = 7
GROUP = 4
GROUPS = PEERS // GROUP
SLOTS = 48
PAIR = 56
WIDTH = 128
TILE = 256
LAGS = 15


def lag_table(times):
    table = np.zeros((times, 128), np.float32)
    t = np.arange(times)
    for lag in range(-7, 8):
        angle = 2.0 * math.pi * ((lag * t) % times) / times
        table[:, 2 * (lag + 7)] = np.cos(angle) / times
        table[:, 2 * (lag + 7) + 1] = np.sin(angle) / times
    return table


SELF = PEERS - 1


def quot(a, b):
    return a // b if isinstance(a, int) else lax.div(a, b)


def mod(a, b):
    return a % b if isinstance(a, int) else lax.rem(a, b)


def offset(group, k):
    half = quot(group, 4)
    return mod(1 + group, 4), 2 + half if k < 2 else 1 - half, 1 - k % 2


def flip8(x):
    rows = lax.broadcasted_iota(jnp.int32, (8, WIDTH), 0)
    return jnp.take_along_axis(x, 7 - rows, axis=0)


def pack(first, second, rank):
    rows = lax.broadcasted_iota(jnp.int32, (8, WIDTH), 0)
    parts = [first[0:8]]
    for v in range(1, 6):
        other = flip8(second[8 * (6 - v) : 8 * (6 - v) + 8])
        parts.append(jnp.where(rows + 8 * v < rank, first[8 * v : 8 * v + 8], other))
    parts.append(flip8(second[0:8]))
    return parts


def unpack(packed, rank):
    rows = lax.broadcasted_iota(jnp.int32, (8, WIDTH), 0)
    first, second = [], []
    for v in range(6):
        first.append(jnp.where(rows + 8 * v < rank, packed[v], 0.0))
        second.append(jnp.where(rows + 8 * v < PAIR - rank, flip8(packed[6 - v]), 0.0))
    return jnp.concatenate(first, axis=0), jnp.concatenate(second, axis=0)


def interleaved(x):
    part = lax.broadcasted_iota(jnp.int32, x.shape, 1) // 32
    by32, by64, by96 = (pltpu.roll(x, shift, 1) for shift in (32, 64, 96))
    straight = jnp.where(part == 1, by96, jnp.where(part == 2, by32, x))
    swapped = jnp.where(part == 0, by64, jnp.where(part == 1, -by32, jnp.where(part == 2, by96, -by64)))
    return straight, swapped


def crossed(x):
    rows = []
    for at in range(0, x.shape[0], 64):
        rows += [-x[at + 32 : at + 64], x[at : at + 32]]
    return jnp.concatenate(rows, axis=0)


def kernel(
    u_hbm, ub_hbm, vb_hbm, ranks_hbm, mask_hbm, table_hbm, out_ref,
    u_buf, ub, vb, ranks, mask, table, weights, lags, prod, side, turns, mixed,
    send_a, recv_a, send_b, recv_b, z_send, z_recv, z_acc, r_acc,
    in_sem, u_sem, v_sem, sent_a, got_a, sent_b, got_b, zs_sem, zr_sem,
):
    me = lax.axis_index("tile")
    fx = lax.axis_index("freq")
    z, y, c = quot(me, 8), mod(quot(me, 2), 4), mod(me, 2)
    zs = [mod(z + d, 4) * 8 for d in range(4)]
    ys = [mod(y + d, 4) * 2 for d in range(4)]
    cs = [c, 1 - c]
    xs = [mod(fx + d, 4) for d in range(4)]
    scope = jax.named_scope

    barrier = pltpu.get_barrier_semaphore()
    for slot in range(SELF):
        dz, dy, dc = offset(slot // GROUP, slot % GROUP)
        pl.semaphore_signal(
            barrier, inc=1, device_id={"tile": zs[dz] + ys[dy] + cs[dc]}, device_id_type=MESH
        )
    for dx in (1, 2, 3):
        pl.semaphore_signal(barrier, inc=1, device_id={"freq": xs[dx]}, device_id_type=MESH)

    copies = [
        pltpu.make_async_copy(u_hbm, u_buf, in_sem.at[0]),
        pltpu.make_async_copy(ranks_hbm, ranks, in_sem.at[1]),
        pltpu.make_async_copy(mask_hbm, mask, in_sem.at[2]),
        pltpu.make_async_copy(table_hbm, table, in_sem.at[3]),
    ]

    def u_copy(dz):
        cut = pl.ds(pl.multiple_of(2 * zs[dz], 16), 16)
        return pltpu.make_async_copy(ub_hbm.at[:, :, cut], ub.at[:, :, cut], u_sem.at[dz])

    def v_copy(dz):
        cut = pl.ds(pl.multiple_of(2 * zs[(4 - dz) % 4], 16), 16)
        return pltpu.make_async_copy(vb_hbm.at[:, cut], vb.at[:, cut], v_sem.at[dz])

    copies[0].start()
    copies[1].start()
    for dz in (1, 2, 3, 0):
        u_copy(dz).start()
    copies[2].start()
    copies[3].start()

    def targets(group):
        spots = []
        for k in range(GROUP):
            dz, dy, dc = offset(group, k)
            spots.append(mod(z + dz, 4) * 8 + mod(y + dy, 4) * 2 + cs[dc])
        return spots

    def sources(group):
        spots = []
        for k in range(GROUP):
            dz, dy, dc = offset(group, k)
            spots.append(mod(z + 4 - dz, 4) * 8 + mod(y + 4 - dy, 4) * 2 + cs[dc])
        return spots

    def ends(chunk):
        at = chunk[1]
        if chunk[0] == 0:
            return send_a.at[at], recv_a.at[at], sent_a.at[at], got_a.at[at]
        return send_b.at[at], recv_b.at[at], sent_b.at[at], got_b.at[at]

    def dispatch(chunk, group, count=GROUP):
        source, landing, sent, got = ends(chunk)
        where = targets(group)
        for k in range(*count) if isinstance(count, tuple) else range(count):
            slot = GROUP * group + k
            pltpu.make_async_remote_copy(
                src_ref=source.at[slot],
                dst_ref=landing.at[slot],
                send_sem=sent,
                recv_sem=got.at[group],
                device_id={"tile": where[k]},
                device_id_type=MESH,
            ).start()

    def dispatch_next(number):
        @pl.when(number < 4 * GROUPS)
        def _():
            chunk, group = (0, lax.div(number, GROUPS)), lax.rem(number, GROUPS)
            dispatch(chunk, group, GROUP - 1)

            @pl.when(group < GROUPS - 1)
            def _():
                dispatch(chunk, group, (GROUP - 1, GROUP))

    def arrive(chunk, group, count=GROUP):
        source, landing, _, got = ends(chunk)
        cut = pl.ds(GROUP * group, count)
        pltpu.make_async_copy(source.at[cut], landing.at[cut], got.at[group]).wait()

    def drain(chunk):
        source, landing, sent, _ = ends(chunk)
        cut = pl.ds(0, SELF)
        pltpu.make_async_copy(source.at[cut], landing.at[cut], sent).wait()

    with scope("u_wait"):
        copies[0].wait()
    for f in range(2):
        for i in range(2):
            x = u_buf[f, 256 * i : 256 * i + 256, :].astype(jnp.float32)
            straight, swapped = interleaved(x)
            weights[f, i, 0:256, :] = straight.astype(jnp.bfloat16)
            weights[f, i, 256:512, :] = swapped.astype(jnp.bfloat16)
    copies[1].wait()

    def multiply(group, tile, weight):
        where = targets(group)
        for i in range(2):
            for f in range(2):
                tiles = [tile(f, i, d) for d in where]
                real = jnp.concatenate([t[0] for t in tiles], axis=0)
                imag = jnp.concatenate([t[1] for t in tiles], axis=0)
                lhs = jnp.concatenate([real, imag], axis=1)
                prod[i, f] = jnp.dot(lhs, weight(f, i), preferred_element_type=jnp.float32)

    def emit(stage, jj, group, rank):
        where = targets(group)
        low = lax.broadcasted_iota(jnp.int32, (8, WIDTH), 1) < WIDTH // 2
        for k in range(GROUP):
            slot = GROUP * group + k
            cut = slice(48 * k, 48 * k + 48)
            top, bottom = (pack(prod[i, 0, cut], prod[i, 1, cut], rank(i, where[k])) for i in range(2))
            if stage == 1:
                send_b[jj, slot] = jnp.concatenate(top + bottom, axis=0).astype(jnp.bfloat16)
                continue
            pairs = list(zip(top, bottom))
            left = [jnp.where(low, t, pltpu.roll(b, WIDTH // 2, 1)) for t, b in pairs]
            right = [jnp.where(low, pltpu.roll(t, WIDTH // 2, 1), b) for t, b in pairs]
            send_a[2 * jj, slot] = jnp.concatenate(left, axis=0).astype(jnp.bfloat16)
            send_a[2 * jj + 1, slot] = jnp.concatenate(right, axis=0).astype(jnp.bfloat16)

    def coefficients(stage, jj, tile, weight, rank, before=None, chunk=None):
        multiply(0, tile, weight)
        emit(stage, jj, 0, rank)
        if before is not None:
            before(1)
            dispatch(chunk, 0)
        multiply(1, tile, weight)

        def step(group, carry):
            if chunk is not None:
                dispatch(chunk, group - 2)
            emit(stage, jj, group - 1, rank)
            multiply(group, tile, weight)
            return carry

        first = 2
        if before is not None:
            before(2)
            emit(stage, jj, 1, rank)
            multiply(2, tile, weight)
            before(3)
            first = 3
        lax.fori_loop(first, GROUPS, step, 0)
        if chunk is not None:
            dispatch(chunk, GROUPS - 2)
        emit(stage, jj, GROUPS - 1, rank)
        if chunk is not None:
            dispatch(chunk, GROUPS - 1, GROUP - 1)

    def adjoint(jj, **marks):
        coefficients(
            0, jj,
            lambda f, i, d: ub[f, i, 2 * d + jj],
            lambda f, i: weights[f, i],
            lambda i, d: ranks[0, 2 * me + i, 2 * d + jj],
            **marks,
        )

    def forward(jj):
        coefficients(
            1, jj,
            lambda f, i, d: vb[f, 2 * d + i, jj],
            lambda f, i: weights[f, 0],
            lambda i, d: ranks[0, 2 * d + i, 2 * me + jj],
            chunk=(1, jj),
        )

    def loaded(group):
        if group == 1:
            with scope("barrier"):
                pl.semaphore_wait(barrier, PEERS - 1 + 3)
            u_copy(2).wait()
        elif group == 2:
            u_copy(3).wait()
        else:
            u_copy(0).wait()
            for dz in (1, 2, 3, 0):
                v_copy(dz).start()

    with scope("adj0"):
        u_copy(1).wait()
        adjoint(0, before=loaded, chunk=(0, 0))
        for group in range(LEAD):
            dispatch((0, 1), group)
    with scope("adj1"):
        adjoint(1)

    copies[2].wait()
    copies[3].wait()
    kept = mask[...].astype(jnp.float32)
    mixing = lax.dot_general(
        kept, table[...], (((0,), (0,)), ((), ())),
        precision=lax.Precision.HIGHEST, preferred_element_type=jnp.float32,
    )
    for lag in range(LAGS):
        for part in range(2):
            column = mixing[:, 2 * lag + part : 2 * lag + part + 1]
            lags[lag, part] = jnp.broadcast_to(column, (64, 128))

    def pieces_of(block, start):
        return [block[start + 8 * v : start + 8 * v + 8] for v in range(7)]

    def slot_of(group, k, last):
        return None if last and k == GROUP - 1 else GROUP * group + k

    def take(chunk, group, last=False):
        jj = chunk[1] // 2
        whence = sources(group)
        low = lax.broadcasted_iota(jnp.int32, (8, WIDTH), 1) < WIDTH // 2
        stacks = [[], []]
        for k in range(GROUP):
            slot = slot_of(group, k, last)
            block = (send_a if slot is None else recv_a)[chunk[1], SELF if slot is None else slot]
            rank = jnp.where(low, *(ranks[0, 2 * whence[k] + i, 2 * me + jj] for i in range(2)))
            pair = unpack(pieces_of(block.astype(jnp.float32), 0), rank)
            for f in range(2):
                stacks[f].append(pair[f].astype(jnp.bfloat16))
        for f in range(2):
            side[f] = jnp.concatenate(stacks[f], axis=0).T

    def add(chunk, group):
        jj = chunk[1] // 2
        whence = sources(group)
        for f in range(2):
            total = z_acc[f]
            for i in range(2):
                held = side[f, 64 * i : 64 * i + 64]
                for c, lhs in enumerate((held, crossed(held))):
                    rhs = jnp.concatenate([vb[f, 2 * d + i, jj, c] for d in whence], axis=0)
                    total = total + jnp.dot(lhs, rhs, preferred_element_type=jnp.float32)
            z_acc[f] = total

    def take_back(chunk, group, last=False):
        jj = chunk[1]
        whence = sources(group)
        stacks = [[[], []], [[], []]]
        for k in range(GROUP):
            slot = slot_of(group, k, last)
            block = (send_b[jj, SELF] if slot is None else recv_b[jj, slot]).astype(jnp.float32)
            for i in range(2):
                pair = unpack(pieces_of(block, PAIR * i), ranks[0, 2 * me + i, 2 * whence[k] + jj])
                for f in range(2):
                    stacks[f][i].append(pair[f].astype(jnp.bfloat16))
        for f in range(2):
            for i in range(2):
                turns[f, i] = jnp.concatenate(stacks[f][i], axis=0).T

    def add_back(chunk, group):
        jj = chunk[1]
        whence = sources(group)
        for f in range(2):
            for i in range(2):
                held = turns[f, i]
                total = r_acc[f, i]
                for c, lhs in enumerate((held, crossed(held))):
                    rhs = jnp.concatenate([ub[f, i, 2 * d + jj, c] for d in whence], axis=0)
                    total = total + jnp.dot(lhs, rhs, preferred_element_type=jnp.float32)
                r_acc[f, i] = total

    def gather(chunk, ahead=False):
        unpack_group, add_group = ((take, add), (take_back, add_back))[chunk[0]]
        arrive(chunk, 0)
        first = (chunk[1] + 1) * GROUPS + LEAD
        if ahead:
            dispatch_next(first + zero)
        unpack_group(chunk, 0)

        def step(group, carry):
            arrive(chunk, group)
            if ahead:
                dispatch_next(first + group)
            add_group(chunk, group - 1)
            unpack_group(chunk, group)
            return carry

        lax.fori_loop(1, GROUPS - 1, step, 0)
        arrive(chunk, GROUPS - 1, GROUP - 1)
        if ahead:
            dispatch_next(first + zero + GROUPS - 1)
        add_group(chunk, GROUPS - 2)
        unpack_group(chunk, GROUPS - 1, True)
        add_group(chunk, GROUPS - 1)

    zero = mod(fx, 1)

    def clear():
        z_acc[...] = jnp.zeros_like(z_acc)

    def z_copy(jj, h, dx):
        return pltpu.make_async_remote_copy(
            src_ref=z_send.at[jj, h],
            dst_ref=z_recv.at[jj, h, dx - 1],
            send_sem=zs_sem.at[jj, h, dx - 1],
            recv_sem=zr_sem.at[jj, h, dx - 1],
            device_id={"freq": xs[dx]},
            device_id_type=MESH,
        )

    def share(jj, h):
        z_send[jj, h] = z_acc[...].astype(jnp.bfloat16)
        for dx in (2, 1, 3):
            z_copy(jj, h, dx).start()
        clear()

    def mix(jj, h):
        with scope(f"mixwait{jj}{h}"):
            for dx in (1, 3, 2):
                z_copy(jj, h, dx).wait_recv()
        rows = slice(32 * h, 32 * h + 32)
        for cut in (slice(0, 128), slice(128, 256)):
            total = [[jnp.zeros((32, 128), jnp.float32) for _ in range(2)] for _ in range(2)]
            for dx in range(4):
                held = z_send.at[jj, h] if dx == 0 else z_recv.at[jj, h, dx - 1]
                for g in range(2):
                    zr = held[g, 0:32, cut].astype(jnp.float32)
                    zi = held[g, 32:64, cut].astype(jnp.float32)
                    for f in range(2):
                        lag = 2 * (xs[(4 - dx) % 4] - fx) + g - f + 7
                        cr = lags[lag, 0, rows]
                        ci = lags[lag, 1, rows]
                        total[f][0] += cr * zr - ci * zi
                        total[f][1] += cr * zi + ci * zr
            for f in range(2):
                mixed[f, 64 * h : 64 * h + 32, cut] = total[f][0]
                mixed[f, 64 * h + 32 : 64 * h + 64, cut] = total[f][1]

    def ready():
        for f in range(2):
            both = mixed[f]
            weights[f, 0, 0:256, :] = both.T.astype(jnp.bfloat16)
            weights[f, 0, 256:512, :] = (-crossed(both)).T.astype(jnp.bfloat16)

    clear()
    r_acc[...] = jnp.zeros_like(r_acc)
    for dz in (1, 2, 3, 0):
        v_copy(dz).wait()
    with scope("gather00"):
        gather((0, 0), True)
        share(0, 0)
    with scope("gather01"):
        gather((0, 1), True)
        share(0, 1)
    with scope("gather10"):
        gather((0, 2), True)
        share(1, 0)
    with scope("mix0"):
        mix(0, 0)
        mix(0, 1)
        ready()
    with scope("forward0"):
        forward(0)
    with scope("gather11"):
        gather((0, 3))
        share(1, 1)
    with scope("mix1"):
        mix(1, 0)
        mix(1, 1)
        ready()
    with scope("forward1"):
        forward(1)
    with scope("finish0"):
        gather((1, 0))
    with scope("finish1"):
        gather((1, 1))
    with scope("tail"):
        for f in range(2):
            for i in range(2):
                x = r_acc[f, i]
                x = jnp.concatenate([x[0:32], x[64:96], x[32:64], x[96:128]], axis=0)
                out_ref[f, 256 * i : 256 * i + 256, :] = x.T.astype(jnp.bfloat16)
        for jj in range(2):
            drain((0, 2 * jj))
            drain((0, 2 * jj + 1))
            drain((1, jj))
        for jj in range(2):
            for h in range(2):
                for dx in (1, 2, 3):
                    z_copy(jj, h, dx).wait_send()


def local(u_data, u_basis, v_basis, ranks, time_mask):
    times = time_mask.shape[0]
    table = jnp.asarray(lag_table(times))
    anywhere = pl.BlockSpec(memory_space=pl.ANY)
    bf16, f32 = jnp.bfloat16, jnp.float32
    return pl.pallas_call(
        kernel,
        out_shape=pltpu.VMEM(u_data.shape, bf16),
        in_specs=[anywhere] * 6,
        out_specs=pl.BlockSpec(memory_space=pltpu.VMEM),
        scratch_shapes=[
            pltpu.VMEM(u_data.shape, bf16),
            pltpu.VMEM(u_basis.shape, bf16),
            pltpu.VMEM(v_basis.shape, bf16),
            pltpu.SMEM(ranks.shape, jnp.int32),
            pltpu.VMEM(time_mask.shape, jnp.int32),
            pltpu.VMEM(table.shape, f32),
            pltpu.VMEM((2, 2, 2 * TILE, WIDTH), bf16),
            pltpu.VMEM((LAGS, 2, 64, 128), f32),
            pltpu.VMEM((2, 2, GROUP * SLOTS, WIDTH), f32),
            pltpu.VMEM((2, WIDTH, GROUP * SLOTS), bf16),
            pltpu.VMEM((2, 2, WIDTH, GROUP * SLOTS), bf16),
            pltpu.VMEM((2, WIDTH, TILE), f32),
            pltpu.VMEM((4, PEERS, PAIR, WIDTH), bf16),
            pltpu.VMEM((4, PEERS, PAIR, WIDTH), bf16),
            pltpu.VMEM((2, PEERS, 2 * PAIR, WIDTH), bf16),
            pltpu.VMEM((2, PEERS, 2 * PAIR, WIDTH), bf16),
            pltpu.VMEM((2, 2, 2, WIDTH // 2, TILE), bf16),
            pltpu.VMEM((2, 2, 3, 2, WIDTH // 2, TILE), bf16),
            pltpu.VMEM((2, WIDTH // 2, TILE), f32),
            pltpu.VMEM((2, 2, WIDTH, TILE), f32),
            pltpu.SemaphoreType.DMA((4,)),
            pltpu.SemaphoreType.DMA((4,)),
            pltpu.SemaphoreType.DMA((4,)),
            pltpu.SemaphoreType.DMA((4,)),
            pltpu.SemaphoreType.DMA((4, GROUPS)),
            pltpu.SemaphoreType.DMA((2,)),
            pltpu.SemaphoreType.DMA((2, GROUPS)),
            pltpu.SemaphoreType.DMA((2, 2, 3)),
            pltpu.SemaphoreType.DMA((2, 2, 3)),
        ],
        compiler_params=pltpu.CompilerParams(
            collective_id=0, has_side_effects=True, vmem_limit_bytes=63 * 1024 * 1024
        ),
        name="fused",
    )(u_data, u_basis, v_basis, ranks, time_mask, table)


def solution(mesh):
    placed = (
        P("freq", "tile", None),
        P("freq", "tile", None, None, None, None),
        P("freq", None, "tile", None, None, None),
        P("freq", None, None),
        P(),
    )
    return jax.shard_map(
        local, mesh=mesh, in_specs=placed, out_specs=P("freq", "tile", None), check_vma=False
    )
```

```python
import math

import jax
import jax.numpy as jnp
import numpy as np
from jax import lax
from jax.experimental import pallas as pl
from jax.experimental.pallas import tpu as pltpu
from jax.sharding import PartitionSpec as P

MESH = pl.DeviceIdType.MESH
PEERS = 32
GROUP = 4
GROUPS = PEERS // GROUP
SLOTS = 48
PAIR = 56
WIDTH = 128
TILE = 256
LAGS = 15


def lag_table(times):
    table = np.zeros((times, 128), np.float32)
    t = np.arange(times)
    for lag in range(-7, 8):
        angle = 2.0 * math.pi * ((lag * t) % times) / times
        table[:, 2 * (lag + 7)] = np.cos(angle) / times
        table[:, 2 * (lag + 7) + 1] = np.sin(angle) / times
    return table


SELF = PEERS - 1


def quot(a, b):
    return a // b if isinstance(a, int) else lax.div(a, b)


def mod(a, b):
    return a % b if isinstance(a, int) else lax.rem(a, b)


def offset(group, k):
    half = quot(group, 4)
    return mod(1 + group, 4), 2 + half if k < 2 else 1 - half, 1 - k % 2


def flip8(x):
    rows = lax.broadcasted_iota(jnp.int32, (8, WIDTH), 0)
    return jnp.take_along_axis(x, 7 - rows, axis=0)


def pack(first, second, rank):
    rows = lax.broadcasted_iota(jnp.int32, (8, WIDTH), 0)
    parts = [first[0:8]]
    for v in range(1, 6):
        other = flip8(second[8 * (6 - v) : 8 * (6 - v) + 8])
        parts.append(jnp.where(rows + 8 * v < rank, first[8 * v : 8 * v + 8], other))
    parts.append(flip8(second[0:8]))
    return parts


def unpack(packed, rank):
    rows = lax.broadcasted_iota(jnp.int32, (8, WIDTH), 0)
    first, second = [], []
    for v in range(6):
        first.append(jnp.where(rows + 8 * v < rank, packed[v], 0.0))
        second.append(jnp.where(rows + 8 * v < PAIR - rank, flip8(packed[6 - v]), 0.0))
    return jnp.concatenate(first, axis=0), jnp.concatenate(second, axis=0)


def interleaved(x):
    part = lax.broadcasted_iota(jnp.int32, x.shape, 1) // 32
    by32, by64, by96 = (pltpu.roll(x, shift, 1) for shift in (32, 64, 96))
    straight = jnp.where(part == 1, by96, jnp.where(part == 2, by32, x))
    swapped = jnp.where(part == 0, by64, jnp.where(part == 1, -by32, jnp.where(part == 2, by96, -by64)))
    return straight, swapped


def crossed(x):
    rows = []
    for at in range(0, x.shape[0], 64):
        rows += [-x[at + 32 : at + 64], x[at : at + 32]]
    return jnp.concatenate(rows, axis=0)


def kernel(
    u_hbm, ub_hbm, vb_hbm, ranks_hbm, mask_hbm, table_hbm, out_ref,
    u_buf, ub, vb, ranks, mask, table, weights, lags, prod, side, turns, mixed,
    send_a, recv_a, send_b, recv_b, z_send, z_recv, z_acc, r_acc,
    in_sem, u_sem, v_sem, sent_a, got_a, sent_b, got_b, zs_sem, zr_sem,
):
    me = lax.axis_index("tile")
    fx = lax.axis_index("freq")
    z, y, c = quot(me, 8), mod(quot(me, 2), 4), mod(me, 2)
    zs = [mod(z + d, 4) * 8 for d in range(4)]
    ys = [mod(y + d, 4) * 2 for d in range(4)]
    cs = [c, 1 - c]
    xs = [mod(fx + d, 4) for d in range(4)]
    scope = jax.named_scope

    barrier = pltpu.get_barrier_semaphore()
    for slot in range(SELF):
        dz, dy, dc = offset(slot // GROUP, slot % GROUP)
        pl.semaphore_signal(
            barrier, inc=1, device_id={"tile": zs[dz] + ys[dy] + cs[dc]}, device_id_type=MESH
        )
    for dx in (1, 2, 3):
        pl.semaphore_signal(barrier, inc=1, device_id={"freq": xs[dx]}, device_id_type=MESH)

    copies = [
        pltpu.make_async_copy(u_hbm, u_buf, in_sem.at[0]),
        pltpu.make_async_copy(ranks_hbm, ranks, in_sem.at[1]),
        pltpu.make_async_copy(mask_hbm, mask, in_sem.at[2]),
        pltpu.make_async_copy(table_hbm, table, in_sem.at[3]),
    ]

    def u_copy(dz):
        cut = pl.ds(pl.multiple_of(2 * zs[dz], 16), 16)
        return pltpu.make_async_copy(ub_hbm.at[:, :, cut], ub.at[:, :, cut], u_sem.at[dz])

    def v_copy(dz):
        cut = pl.ds(pl.multiple_of(2 * zs[(4 - dz) % 4], 16), 16)
        return pltpu.make_async_copy(vb_hbm.at[:, cut], vb.at[:, cut], v_sem.at[dz])

    copies[0].start()
    copies[1].start()
    for dz in (1, 2, 3, 0):
        u_copy(dz).start()
    copies[2].start()
    copies[3].start()

    def targets(group, hand=1):
        spots = []
        for k in range(GROUP):
            dz, dy, dc = offset(group, k)
            spots.append(mod(z + 4 + hand * dz, 4) * 8 + mod(y + 4 + hand * dy, 4) * 2 + cs[dc])
        return spots

    def sources(group, hand=1):
        spots = []
        for k in range(GROUP):
            dz, dy, dc = offset(group, k)
            spots.append(mod(z + 4 - hand * dz, 4) * 8 + mod(y + 4 - hand * dy, 4) * 2 + cs[dc])
        return spots

    def ends(chunk):
        at = chunk[1]
        if chunk[0] == 0:
            return send_a.at[at], recv_a.at[at], sent_a.at[at], got_a.at[at]
        return send_b.at[at], recv_b.at[at], sent_b.at[at], got_b.at[at]

    def dispatch(chunk, group, count=GROUP):
        source, landing, sent, got = ends(chunk)
        where = targets(group, 1 - 2 * chunk[0])
        for k in range(*count) if isinstance(count, tuple) else range(count):
            slot = GROUP * group + k
            pltpu.make_async_remote_copy(
                src_ref=source.at[slot],
                dst_ref=landing.at[slot],
                send_sem=sent,
                recv_sem=got.at[group],
                device_id={"tile": where[k]},
                device_id_type=MESH,
            ).start()

    def dispatch_next(number):
        chunk, group = (0, lax.div(number, GROUPS)), lax.rem(number, GROUPS)
        dispatch(chunk, group, GROUP - 1)

        @pl.when(group < GROUPS - 1)
        def _():
            dispatch(chunk, group, (GROUP - 1, GROUP))

    def arrive(chunk, group, count=GROUP):
        source, landing, _, got = ends(chunk)
        cut = pl.ds(GROUP * group, count)
        pltpu.make_async_copy(source.at[cut], landing.at[cut], got.at[group]).wait()

    def drain(chunk):
        source, landing, sent, _ = ends(chunk)
        cut = pl.ds(0, SELF)
        pltpu.make_async_copy(source.at[cut], landing.at[cut], sent).wait()

    with scope("u_wait"):
        copies[0].wait()
    for f in range(2):
        for i in range(2):
            x = u_buf[f, 256 * i : 256 * i + 256, :].astype(jnp.float32)
            straight, swapped = interleaved(x)
            weights[f, i, 0:256, :] = straight.astype(jnp.bfloat16)
            weights[f, i, 256:512, :] = swapped.astype(jnp.bfloat16)
    copies[1].wait()

    def multiply(stage, group, tile, weight):
        where = targets(group, 1 - 2 * stage)
        for i in range(2):
            for f in range(2):
                tiles = [tile(f, i, d) for d in where]
                real = jnp.concatenate([t[0] for t in tiles], axis=0)
                imag = jnp.concatenate([t[1] for t in tiles], axis=0)
                lhs = jnp.concatenate([real, imag], axis=1)
                prod[i, f] = jnp.dot(lhs, weight(f, i), preferred_element_type=jnp.float32)

    def emit(stage, jj, group, rank):
        where = targets(group, 1 - 2 * stage)
        low = lax.broadcasted_iota(jnp.int32, (8, WIDTH), 1) < WIDTH // 2
        for k in range(GROUP):
            slot = GROUP * group + k
            cut = slice(48 * k, 48 * k + 48)
            top, bottom = (pack(prod[i, 0, cut], prod[i, 1, cut], rank(i, where[k])) for i in range(2))
            if stage == 1:
                send_b[jj, slot] = jnp.concatenate(top + bottom, axis=0).astype(jnp.bfloat16)
                continue
            pairs = list(zip(top, bottom))
            left = [jnp.where(low, t, pltpu.roll(b, WIDTH // 2, 1)) for t, b in pairs]
            right = [jnp.where(low, pltpu.roll(t, WIDTH // 2, 1), b) for t, b in pairs]
            send_a[2 * jj, slot] = jnp.concatenate(left, axis=0).astype(jnp.bfloat16)
            send_a[2 * jj + 1, slot] = jnp.concatenate(right, axis=0).astype(jnp.bfloat16)

    def coefficients(stage, jj, tile, weight, rank, before=None, chunk=None):
        multiply(stage, 0, tile, weight)
        emit(stage, jj, 0, rank)
        if before is not None:
            before(1)
        if chunk is not None:
            dispatch(chunk, 0)
        multiply(stage, 1, tile, weight)

        if before is not None:
            before(2)
        emit(stage, jj, 1, rank)
        multiply(stage, 2, tile, weight)
        if before is not None:
            before(3)

        def step(group, carry):
            if chunk is not None:
                dispatch(chunk, group - 2)
            emit(stage, jj, group - 1, rank)
            multiply(stage, group, tile, weight)
            return carry

        lax.fori_loop(3, GROUPS, step, 0)
        if chunk is not None:
            dispatch(chunk, GROUPS - 2)
        emit(stage, jj, GROUPS - 1, rank)
        if chunk is not None:
            dispatch(chunk, GROUPS - 1, GROUP - 1)

    def adjoint(jj, **marks):
        coefficients(
            0, jj,
            lambda f, i, d: ub[f, i, 2 * d + jj],
            lambda f, i: weights[f, i],
            lambda i, d: ranks[0, 2 * me + i, 2 * d + jj],
            **marks,
        )

    def forward(jj):
        coefficients(
            1, jj,
            lambda f, i, d: vb[f, 2 * d + i, jj],
            lambda f, i: weights[f, 0],
            lambda i, d: ranks[0, 2 * d + i, 2 * me + jj],
            chunk=(1, jj),
        )

    def loaded(group):
        if group == 1:
            with scope("barrier"):
                pl.semaphore_wait(barrier, PEERS - 1 + 3)
            u_copy(2).wait()
        elif group == 2:
            u_copy(3).wait()
        else:
            u_copy(0).wait()
            for dz in (1, 2, 3, 0):
                v_copy(dz).start()

    with scope("adj0"):
        u_copy(1).wait()
        adjoint(0, before=loaded, chunk=(0, 0))
        for group in range(GROUPS):
            dispatch((0, 1), group, GROUP - (group == GROUPS - 1))
    with scope("adj1"):
        adjoint(1)

    copies[2].wait()
    copies[3].wait()
    kept = mask[...].astype(jnp.float32)
    mixing = lax.dot_general(
        kept, table[...], (((0,), (0,)), ((), ())),
        precision=lax.Precision.HIGHEST, preferred_element_type=jnp.float32,
    )
    for lag in range(LAGS):
        for part in range(2):
            column = mixing[:, 2 * lag + part : 2 * lag + part + 1]
            lags[lag, part] = jnp.broadcast_to(column, (64, 128))

    def pieces_of(block, start):
        return [block[start + 8 * v : start + 8 * v + 8] for v in range(7)]

    def slot_of(group, k, last):
        return None if last and k == GROUP - 1 else GROUP * group + k

    def take(chunk, group, last=False):
        jj = chunk[1] // 2
        whence = sources(group)
        low = lax.broadcasted_iota(jnp.int32, (8, WIDTH), 1) < WIDTH // 2
        stacks = [[], []]
        for k in range(GROUP):
            slot = slot_of(group, k, last)
            block = (send_a if slot is None else recv_a)[chunk[1], SELF if slot is None else slot]
            rank = jnp.where(low, *(ranks[0, 2 * whence[k] + i, 2 * me + jj] for i in range(2)))
            pair = unpack(pieces_of(block.astype(jnp.float32), 0), rank)
            for f in range(2):
                stacks[f].append(pair[f].astype(jnp.bfloat16))
        for f in range(2):
            side[f] = jnp.concatenate(stacks[f], axis=0).T

    def add(chunk, group):
        jj = chunk[1] // 2
        whence = sources(group)
        for f in range(2):
            total = z_acc[f]
            for i in range(2):
                held = side[f, 64 * i : 64 * i + 64]
                for c, lhs in enumerate((held, crossed(held))):
                    rhs = jnp.concatenate([vb[f, 2 * d + i, jj, c] for d in whence], axis=0)
                    total = total + jnp.dot(lhs, rhs, preferred_element_type=jnp.float32)
            z_acc[f] = total

    def take_back(chunk, group, last=False):
        jj = chunk[1]
        whence = sources(group, -1)
        stacks = [[[], []], [[], []]]
        for k in range(GROUP):
            slot = slot_of(group, k, last)
            block = (send_b[jj, SELF] if slot is None else recv_b[jj, slot]).astype(jnp.float32)
            for i in range(2):
                pair = unpack(pieces_of(block, PAIR * i), ranks[0, 2 * me + i, 2 * whence[k] + jj])
                for f in range(2):
                    stacks[f][i].append(pair[f].astype(jnp.bfloat16))
        for f in range(2):
            for i in range(2):
                turns[f, i] = jnp.concatenate(stacks[f][i], axis=0).T

    def add_back(chunk, group):
        jj = chunk[1]
        whence = sources(group, -1)
        for f in range(2):
            for i in range(2):
                held = turns[f, i]
                total = r_acc[f, i]
                for c, lhs in enumerate((held, crossed(held))):
                    rhs = jnp.concatenate([ub[f, i, 2 * d + jj, c] for d in whence], axis=0)
                    total = total + jnp.dot(lhs, rhs, preferred_element_type=jnp.float32)
                r_acc[f, i] = total

    def gather(chunk, first=0, stop=GROUPS, follow=None):
        unpack_group, add_group = ((take, add), (take_back, add_back))[chunk[0]]
        if first == 0:
            arrive(chunk, 0)
            if follow is not None:
                follow(zero)
            unpack_group(chunk, 0)
            first = 1

        def step(group, carry):
            arrive(chunk, group)
            if follow is not None:
                follow(group)
            add_group(chunk, group - 1)
            unpack_group(chunk, group)
            return carry

        lax.fori_loop(first, min(stop, GROUPS - 1), step, 0)
        if stop == GROUPS:
            arrive(chunk, GROUPS - 1, GROUP - 1)
            if follow is not None:
                follow(zero + GROUPS - 1)
            add_group(chunk, GROUPS - 2)
            unpack_group(chunk, GROUPS - 1, True)
            add_group(chunk, GROUPS - 1)

    zero = mod(fx, 1)

    def two_more(group):
        dispatch_next(2 * GROUPS + 2 * group)
        dispatch_next(2 * GROUPS + 2 * group + 1)

    def one_more(first):
        return lambda group: dispatch_next(first + group)

    def clear():
        z_acc[...] = jnp.zeros_like(z_acc)

    def z_copy(jj, h, dx):
        return pltpu.make_async_remote_copy(
            src_ref=z_send.at[jj, h],
            dst_ref=z_recv.at[jj, h, dx - 1],
            send_sem=zs_sem.at[jj, h, dx - 1],
            recv_sem=zr_sem.at[jj, h, dx - 1],
            device_id={"freq": xs[dx]},
            device_id_type=MESH,
        )

    def share(jj, h):
        z_send[jj, h] = z_acc[...].astype(jnp.bfloat16)
        for dx in (2, 1, 3):
            z_copy(jj, h, dx).start()
        clear()

    def mix(jj, h):
        with scope(f"mixwait{jj}{h}"):
            for dx in (1, 3, 2):
                z_copy(jj, h, dx).wait_recv()
        rows = slice(32 * h, 32 * h + 32)
        for cut in (slice(0, 128), slice(128, 256)):
            total = [[jnp.zeros((32, 128), jnp.float32) for _ in range(2)] for _ in range(2)]
            for dx in range(4):
                held = z_send.at[jj, h] if dx == 0 else z_recv.at[jj, h, dx - 1]
                for g in range(2):
                    zr = held[g, 0:32, cut].astype(jnp.float32)
                    zi = held[g, 32:64, cut].astype(jnp.float32)
                    for f in range(2):
                        lag = 2 * (xs[(4 - dx) % 4] - fx) + g - f + 7
                        cr = lags[lag, 0, rows]
                        ci = lags[lag, 1, rows]
                        total[f][0] += cr * zr - ci * zi
                        total[f][1] += cr * zi + ci * zr
            for f in range(2):
                mixed[f, 64 * h : 64 * h + 32, cut] = total[f][0]
                mixed[f, 64 * h + 32 : 64 * h + 64, cut] = total[f][1]

    def ready():
        for f in range(2):
            both = mixed[f]
            weights[f, 0, 0:256, :] = both.T.astype(jnp.bfloat16)
            weights[f, 0, 256:512, :] = (-crossed(both)).T.astype(jnp.bfloat16)

    clear()
    r_acc[...] = jnp.zeros_like(r_acc)
    for dz in (1, 2, 3, 0):
        v_copy(dz).wait()
    with scope("gather00"):
        gather((0, 0), follow=one_more(2 * GROUPS))
        share(0, 0)
    with scope("gather01"):
        gather((0, 1), follow=one_more(3 * GROUPS))
        share(0, 1)
    with scope("gather10a"):
        gather((0, 2), 0, 8)
        share(1, 0)
    with scope("mix0"):
        mix(0, 0)
        mix(0, 1)
        ready()
    with scope("forward0"):
        forward(0)
    with scope("gather11"):
        gather((0, 3))
        share(1, 1)
    with scope("mix1"):
        mix(1, 0)
        mix(1, 1)
        ready()
    with scope("forward1"):
        forward(1)
    with scope("finish0"):
        gather((1, 0))
    with scope("finish1"):
        gather((1, 1))
    with scope("tail"):
        for f in range(2):
            for i in range(2):
                x = r_acc[f, i]
                x = jnp.concatenate([x[0:32], x[64:96], x[32:64], x[96:128]], axis=0)
                out_ref[f, 256 * i : 256 * i + 256, :] = x.T.astype(jnp.bfloat16)
        for jj in range(2):
            drain((0, 2 * jj))
            drain((0, 2 * jj + 1))
            drain((1, jj))
        for jj in range(2):
            for h in range(2):
                for dx in (1, 2, 3):
                    z_copy(jj, h, dx).wait_send()


def local(u_data, u_basis, v_basis, ranks, time_mask):
    times = time_mask.shape[0]
    table = jnp.asarray(lag_table(times))
    anywhere = pl.BlockSpec(memory_space=pl.ANY)
    bf16, f32 = jnp.bfloat16, jnp.float32
    return pl.pallas_call(
        kernel,
        out_shape=pltpu.VMEM(u_data.shape, bf16),
        in_specs=[anywhere] * 6,
        out_specs=pl.BlockSpec(memory_space=pltpu.VMEM),
        scratch_shapes=[
            pltpu.VMEM(u_data.shape, bf16),
            pltpu.VMEM(u_basis.shape, bf16),
            pltpu.VMEM(v_basis.shape, bf16),
            pltpu.SMEM(ranks.shape, jnp.int32),
            pltpu.VMEM(time_mask.shape, jnp.int32),
            pltpu.VMEM(table.shape, f32),
            pltpu.VMEM((2, 2, 2 * TILE, WIDTH), bf16),
            pltpu.VMEM((LAGS, 2, 64, 128), f32),
            pltpu.VMEM((2, 2, GROUP * SLOTS, WIDTH), f32),
            pltpu.VMEM((2, WIDTH, GROUP * SLOTS), bf16),
            pltpu.VMEM((2, 2, WIDTH, GROUP * SLOTS), bf16),
            pltpu.VMEM((2, WIDTH, TILE), f32),
            pltpu.VMEM((4, PEERS, PAIR, WIDTH), bf16),
            pltpu.VMEM((4, PEERS, PAIR, WIDTH), bf16),
            pltpu.VMEM((2, PEERS, 2 * PAIR, WIDTH), bf16),
            pltpu.VMEM((2, PEERS, 2 * PAIR, WIDTH), bf16),
            pltpu.VMEM((2, 2, 2, WIDTH // 2, TILE), bf16),
            pltpu.VMEM((2, 2, 3, 2, WIDTH // 2, TILE), bf16),
            pltpu.VMEM((2, WIDTH // 2, TILE), f32),
            pltpu.VMEM((2, 2, WIDTH, TILE), f32),
            pltpu.SemaphoreType.DMA((4,)),
            pltpu.SemaphoreType.DMA((4,)),
            pltpu.SemaphoreType.DMA((4,)),
            pltpu.SemaphoreType.DMA((4,)),
            pltpu.SemaphoreType.DMA((4, GROUPS)),
            pltpu.SemaphoreType.DMA((2,)),
            pltpu.SemaphoreType.DMA((2, GROUPS)),
            pltpu.SemaphoreType.DMA((2, 2, 3)),
            pltpu.SemaphoreType.DMA((2, 2, 3)),
        ],
        compiler_params=pltpu.CompilerParams(
            collective_id=0, has_side_effects=True, vmem_limit_bytes=63 * 1024 * 1024
        ),
        name="fused",
    )(u_data, u_basis, v_basis, ranks, time_mask, table)


def solution(mesh):
    placed = (
        P("freq", "tile", None),
        P("freq", "tile", None, None, None, None),
        P("freq", None, "tile", None, None, None),
        P("freq", None, None),
        P(),
    )
    return jax.shard_map(
        local, mesh=mesh, in_specs=placed, out_specs=P("freq", "tile", None), check_vma=False
    )
```
